128 devices in a mesh: section: 16 (over y, z), dom: 8 (over x, core).
Axes of the slice: x: 4, y: 4, z: 4, core: 2. Of those that a mesh axis runs over, the one named last changes fastest.
Arguments:
- features: bfloat16 [12, 2048, 256], P(None, 'dom'), may hold values from -6 to 6
- cotangent: bfloat16 [12, 2048, 256], P(None, 'dom'), may hold values from -3 to 3
- weights: bfloat16 [16, 256, 256], P('section'), may hold values from -0.375 to 0.375
- tiles: bfloat16 [16, 6, 128, 128], P('dom'), may hold values from 0.0005 to 1
- sources: int32 [16, 6], P('dom'), may hold values from 0 to 15, as said below
- counts: int32 [16], P('dom'), may hold values from 1 to 6
Outputs:
- weight_grads: float32 [16, 256, 256], P('section')
The draws below stay inside these ranges and needn't reach their ends.
Inputs may be any that keep to these rules, and one draw needn't show every extreme that they name: `sources`: entry 0 of each block's list is the block itself; every entry, used or not, names a block that lies on the same index of dom or is the block just before or just after that index's blocks.
All inputs are finite; a program needn't handle non-finite values.
Results may differ from the reference program's by a relative error of at most 0.02.
Values may be sent and summed in bfloat16 or wider, within the bound.
A program may use at most 64 MiB of HBM per device.

```python
import math
import jax
import jax.numpy as jnp
from jax import lax

HID = 256
BS = 128
KNB = 6
BLK_DEV = 2
MB = 12
LAYERS = 16
NBLK = 16
NODES = 2048
N_DOM = 8


def draw_sources(key, part):
    blocks = jnp.arange(NBLK)
    device = blocks // BLK_DEV
    place = blocks % BLK_DEV
    lowest = jnp.maximum(device * BLK_DEV - 1, 0)
    highest = jnp.minimum((device + 1) * BLK_DEV + 1, NBLK)
    picks = jax.random.randint(key, (NBLK, KNB), 0, 1 << 20)
    chosen = lowest[:, None] + picks % (highest - lowest)[:, None]
    left_edge = (place == 0) & (device > 0)
    right_edge = (place == BLK_DEV - 1) & (device < N_DOM - 1)
    second = jnp.where(left_edge, blocks - 1, jnp.where(right_edge, blocks + 1, chosen[:, 1]))
    chosen = chosen.at[:, 1].set(second).at[:, 0].set(blocks)
    return chosen.astype(jnp.int32)


def draw_counts(key, part):
    blocks = jnp.arange(NBLK)
    device = blocks // BLK_DEV
    place = blocks % BLK_DEV
    edge = (place == 0) & (device > 0) | (place == BLK_DEV - 1) & (device < N_DOM - 1)
    drawn = jax.random.randint(key, (NBLK,), 1, KNB + 1)
    drawn = jnp.where(edge, jnp.maximum(drawn, 2), drawn)
    drawn = drawn.at[0].set(1).at[NBLK - 1].set(KNB)
    return drawn.astype(jnp.int32)


def draw_tiles(key, part):
    base = jax.random.fold_in(key, 71)
    key_diag, key_back = jax.random.split(base)
    shape = (NBLK, KNB, BS, BS)
    diag = jax.random.uniform(key_diag, (NBLK, KNB, BS), jnp.float32, 0.4, 1.0)
    low = jnp.log(jnp.float32(0.0005))
    high = jnp.log(jnp.float32(0.005))
    back = jnp.exp(jax.random.uniform(key_back, shape, jnp.float32, 0.0, 1.0) * (high - low) + low)
    eye = jnp.arange(BS)[:, None] == jnp.arange(BS)[None, :]
    tiles = jnp.where(eye[None, None, :, :], diag[:, :, :, None], back)
    return tiles.astype(jnp.bfloat16)


def draw_cotangent(key, part):
    base = jax.random.fold_in(key, 83)
    shape = (MB, NODES, HID)
    values = jnp.clip(jax.random.normal(base, shape, jnp.float32), -3.0, 3.0)
    return values.astype(jnp.bfloat16)


def block_scale(rng, dims, pieces, smallest, largest):
    loudness = 1.0
    for axis_at, parts in pieces:
        steps = jax.random.uniform(jax.random.fold_in(jax.random.fold_in(rng, 6), axis_at), (parts,), jnp.float32, smallest / len(pieces), largest / len(pieces))
        loudness = loudness * jnp.repeat(jnp.exp(steps), dims[axis_at] // parts).reshape((-1,) + (1,) * (len(dims) - 1 - axis_at))
    return loudness


def bell_draw(key, dims, width, reach, cuts=(), held_as=jnp.bfloat16):
    result = width * jax.random.normal(key, dims, jnp.float32)
    if cuts:
        result = result * block_scale(key, dims, cuts, -0.22, 0.18)
    return jnp.clip(result, -reach, reach).astype(held_as)


def setup_inputs(seed: int = 0) -> dict:
    seeds = jax.random.split(jax.random.key(seed), 7)
    return {
        "features": bell_draw(seeds[0], (MB, NODES, HID), 1.0, 6.0, ((1, 8),)),
        "cotangent": draw_cotangent(jax.random.fold_in(seeds[6], 71), 0),
        "weights": bell_draw(seeds[2], (LAYERS, HID, HID), HID ** -0.5, 0.375, ((0, 16),)),
        "tiles": draw_tiles(jax.random.fold_in(seeds[6], 71), 0),
        "sources": draw_sources(jax.random.fold_in(seeds[6], 71), 0),
        "counts": draw_counts(jax.random.fold_in(seeds[6], 71), 0),
    }


epsilon = 1e-06

def reference(features, cotangent, weights, tiles, sources, counts):
    used = (jnp.arange(KNB)[None, :] < counts[:, None]).astype(jnp.bfloat16)
    masked = tiles * used[:, :, None, None]
    wide = masked.astype(jnp.float32)
    degree = lax.optimization_barrier(jnp.sum(wide, axis=(1, 3)))

    def aggregate(hidden):
        picked = hidden.reshape(NBLK, BS, HID)[sources].astype(jnp.float32)
        summed = jnp.einsum('bkij,bkjh->bih', wide, picked)
        return (summed / degree[:, :, None]).reshape(NODES, HID)

    def normalize(agg):
        scale = lax.rsqrt(lax.optimization_barrier(jnp.mean(agg * agg, axis=-1, keepdims=True)) + epsilon)
        return ((agg * scale).astype(jnp.bfloat16), scale)
    grads = [jnp.zeros((HID, HID), jnp.float32) for layer in range(LAYERS)]
    for snap in range(MB):
        hidden = features[snap]
        inputs = []
        for layer in range(LAYERS):
            inputs.append(hidden)
            agg = aggregate(hidden)
            nrm, scale = normalize(agg)
            z_val = jnp.dot(nrm, weights[layer], preferred_element_type=jnp.float32)
            hidden = (hidden.astype(jnp.float32) + jax.nn.silu(z_val)).astype(jnp.bfloat16)
        grad_bf = cotangent[snap]
        for layer in range(LAYERS - 1, -1, -1):
            agg = aggregate(inputs[layer])
            nrm, scale = normalize(agg)
            z_val = jnp.dot(nrm, weights[layer], preferred_element_type=jnp.float32)
            grad = grad_bf.astype(jnp.float32)
            sig = jax.nn.sigmoid(z_val)
            dz_val = (grad * sig * (1.0 + z_val * (1.0 - sig))).astype(jnp.bfloat16)
            grads[layer] = grads[layer] + jnp.dot(nrm.T, dz_val, preferred_element_type=jnp.float32)
            dnrm = jnp.dot(dz_val, weights[layer].T, preferred_element_type=jnp.float32)
            dagg = scale * (dnrm - agg * scale * scale * lax.optimization_barrier(jnp.mean(dnrm * agg, axis=-1, keepdims=True)))
            dsum = (dagg.reshape(NBLK, BS, HID) / degree[:, :, None]).astype(jnp.bfloat16)
            dpicked = jnp.einsum('bkij,bih->bkjh', wide, dsum.astype(jnp.float32))
            contrib = jnp.zeros((NBLK, BS, HID), jnp.float32).at[sources.reshape(-1)].add(dpicked.reshape(NBLK * KNB, BS, HID))
            grad_bf = (grad + contrib.reshape(NODES, HID)).astype(jnp.bfloat16)
    return jnp.stack(grads) * (1.0 / math.sqrt(MB * NODES))
```

```python
import functools
import math

import jax
import jax.numpy as jnp
from jax import lax
from jax.experimental import pallas as pl
from jax.experimental.pallas import tpu as pltpu
from jax.sharding import PartitionSpec as P

EPSILON = 1e-06
MESH = pl.DeviceIdType.MESH
F32 = jnp.float32
BF16 = jnp.bfloat16

BS = 128
PAIR = 2 * BS
WIN = 4 * BS
HALF = 4
ROWS = HALF * PAIR


def mm(a, b):
    return jnp.dot(a, b, preferred_element_type=F32)


def mm_tn(a, b):
    return lax.dot_general(a, b, (((0,), (0,)), ((), ())), preferred_element_type=F32)


def mm_nt(a, b):
    return lax.dot_general(a, b, (((1,), (1,)), ((), ())), preferred_element_type=F32)


def rows(p, offset=0, size=PAIR):
    return pl.ds(p * PAIR + offset, size)


def kernel(
    scaling, snaps, layers,
    src_ref, cnt_ref, tiles_ref, w_ref, feat_ref, cot_ref, out_ref,
    asend, abuf, atbuf, wbuf, hbuf, cotb, gbuf, nrmb, dsb, scb,
    gsend, grecv, dwst, dwrecv, outg,
    f_send, f_recv, w_send, w_recv, a_send, a_recv, c_send, c_recv,
    h_send, h_recv, g_send, g_recv, d_send, d_recv, o_send, o_recv,
):
    sec = lax.axis_index("section")
    dom = lax.axis_index("dom")
    x, core = dom // 2, dom % 2
    active = sec < snaps
    host_x = lax.rem(sec // 4 + lax.rem(sec, 4), 4)
    is_host = jnp.logical_and(active, x == host_x)
    half = dom // 4
    mirrored = half == 0
    place = jnp.where(mirrored, 3 - dom, dom - 4)
    target = host_x * 2 + half
    other = host_x * 2 + 1 - half
    partner = x * 2 + 1 - core
    slots = [jnp.where(mirrored, 1 - j, j) for j in range(2)]

    def push(src, dst, send, recv, to_sec, to_dom, guard):
        here = jnp.logical_and(to_sec == sec, to_dom == dom)

        @pl.when(jnp.logical_and(guard, here))
        def _():
            pltpu.make_async_copy(src, dst, recv).start()

        @pl.when(jnp.logical_and(guard, jnp.logical_not(here)))
        def _():
            pltpu.make_async_remote_copy(
                src_ref=src, dst_ref=dst, send_sem=send, recv_sem=recv,
                device_id=(to_sec, to_dom), device_id_type=MESH,
            ).start()

    def sent(src, dst, send, recv, to_sec, to_dom, guard):
        here = jnp.logical_and(to_sec == sec, to_dom == dom)

        @pl.when(jnp.logical_and(guard, jnp.logical_not(here)))
        def _():
            pltpu.make_async_remote_copy(
                src_ref=src, dst_ref=dst, send_sem=send, recv_sem=recv,
                device_id=(to_sec, to_dom), device_id_type=MESH,
            ).wait_send()

    def arrived(src, dst, recv):
        pltpu.make_async_copy(src, dst, recv).wait()

    def block(q):
        return pl.ds(pl.multiple_of(q * BS, BS), BS)

    gifts = []
    for j in range(2):
        q = 2 * place + slots[j]
        gifts.append((
            feat_ref.at[jnp.minimum(sec, snaps - 1), pl.ds(j * BS, BS)], hbuf.at[0, block(q + 1)],
            f_send.at[j], f_recv.at[q], sec, target, active,
        ))
    edge = jnp.where(mirrored, 1, 0)
    gifts.append((
        feat_ref.at[jnp.minimum(sec, snaps - 1), block(edge)], hbuf.at[0, pl.ds(0, BS)],
        f_send.at[2], f_recv.at[8], sec, other,
        jnp.logical_and(active, jnp.logical_or(dom == 3, dom == 4)),
    ))
    for gift in gifts:
        push(*gift)
    cots = []
    for j in range(2):
        q = 2 * place + slots[j]
        cots.append((
            cot_ref.at[jnp.minimum(sec, snaps - 1), pl.ds(j * BS, BS)], cotb.at[block(q)],
            c_send.at[j], c_recv.at[q], sec, target, active,
        ))

    lends = []
    for j in range(3):
        to_sec = 4 * j + lax.rem(x - j + 4, 4)
        lends.append((
            w_ref.at[0], wbuf.at[sec], w_send.at[j], w_recv.at[sec], to_sec, dom, True,
        ))
    for lend in lends:
        push(*lend)

    adj = (asend, abuf.at[place], a_send, a_recv.at[place], sec, target, active)

    @pl.when(active)
    def _():
        first = 2 * dom - 1
        for b in range(2):
            want = []
            for k in range(6):
                loc = src_ref[b, k] - first
                loc = jnp.where(mirrored, 3 - loc, loc)
                want.append(jnp.where(k < cnt_ref[b], loc, -1))
            parts = []
            for c in range(4):
                total = jnp.zeros((BS, BS), F32)
                for k in range(6):
                    keep = jnp.where(want[k] == c, 1.0, 0.0).astype(F32)
                    total = total + tiles_ref[b, k].astype(F32) * keep
                parts.append(total)
            degree = jnp.sum(parts[0] + parts[1] + parts[2] + parts[3], axis=-1, keepdims=True)
            scale = 1.0 / degree
            for c in range(4):
                asend[block(slots[b]), pl.ds(c * BS, BS)] = (parts[c] * scale).astype(BF16)

    push(*adj)
    for cot in cots:
        push(*cot)

    @pl.when(is_host)
    def _():
        for s in range(2):
            hbuf[s, pl.ds(ROWS + BS, BS)] = jnp.zeros((BS, hbuf.shape[2]), BF16)
        for q in range(9):
            dst = hbuf.at[0, pl.ds((q + 1) % 9 * BS, BS)]
            arrived(dst, dst, f_recv.at[q])
        for p in range(HALF):
            arrived(abuf.at[p], abuf.at[p], a_recv.at[p])

        def halo(slot):
            return pltpu.make_async_remote_copy(
                src_ref=hbuf.at[slot, pl.ds(BS, BS)], dst_ref=hbuf.at[slot, pl.ds(0, BS)],
                send_sem=h_send.at[slot], recv_sem=h_recv.at[slot],
                device_id=(sec, partner), device_id_type=MESH,
            )

        def forward(layer, last):
            now = lax.rem(layer, 2)
            later = 1 - now
            arrived(wbuf.at[layer], wbuf.at[layer], w_recv.at[layer])
            if last:
                halo(now).wait_recv()
            else:

                @pl.when(layer > 0)
                def _():
                    halo(now).wait_recv()

            for p in range(HALF):
                agg = mm(abuf[p], hbuf[now, pl.ds(p * PAIR, WIN)])
                scale = lax.rsqrt(jnp.mean(agg * agg, axis=-1, keepdims=True) + EPSILON)
                nrm = (agg * scale).astype(BF16)
                nrmb[layer, rows(p)] = nrm
                scb[layer, rows(p)] = jnp.broadcast_to(scale, (PAIR, 128))
                hz = 0.5 * mm(nrm, wbuf[layer])
                t = jnp.tanh(hz)
                u = 1.0 + t
                dsb[layer, rows(p)] = (0.5 * u) * (1.0 + hz * (1.0 - t))
                if not last:
                    old = hbuf[now, rows(p, BS)].astype(F32)
                    hbuf[later, rows(p, BS)] = (old + hz * u).astype(BF16)
                    if p == 0:
                        halo(later).start()
            if not last:
                halo(later).wait_send()

        def forward_step(layer, carry):
            forward(layer, False)
            return carry

        lax.fori_loop(0, layers - 1, forward_step, 0)
        forward(layers - 1, True)

        for p in range(HALF):
            atbuf[p] = abuf[p].T
        for q in range(8):
            arrived(cotb.at[pl.ds(q * BS, BS)], cotb.at[pl.ds(q * BS, BS)], c_recv.at[q])
        gbuf[...] = cotb[...].astype(F32)

        giver = sec * 2 + core

        def rim(slot):
            return pltpu.make_async_remote_copy(
                src_ref=gsend.at[slot], dst_ref=grecv.at[slot],
                send_sem=g_send.at[slot], recv_sem=g_recv.at[slot],
                device_id=(sec, partner), device_id_type=MESH,
            )

        def shares(layer, slot):
            return [
                (
                    dwst.at[slot, pl.ds(e * 32, 32)], dwrecv.at[giver],
                    d_send.at[slot, e], d_recv.at[giver], layer, e, True,
                )
                for e in range(8)
            ]

        def backward(layer, last):
            slot = lax.rem(layer, 2)
            total = None
            daggs = []
            for p in range(HALF):
                dz = (gbuf[rows(p)] * dsb[layer, rows(p)]).astype(BF16)
                nrm = nrmb[layer, rows(p)]
                if not last:
                    dnrm = mm_nt(dz, wbuf[layer])
                    wide = nrm.astype(F32)
                    mean = jnp.mean(dnrm * wide, axis=-1, keepdims=True)
                    scale = scb[layer, rows(p)][:, :1]
                    dagg = (scale * (dnrm - wide * mean)).astype(BF16)
                    daggs.append(dagg)
                    if p == 0:
                        gsend[slot] = mm(atbuf[0, pl.ds(0, BS)], dagg).astype(BF16)
                        rim(slot).start()
                term = mm_tn(nrm, dz)
                total = term if total is None else total + term
            if not last:
                spread = [mm(atbuf[0, pl.ds(BS, WIN - BS)], daggs[0])]
                spread += [mm(atbuf[p], daggs[p]) for p in range(1, HALF)]
                for p in range(HALF):
                    lo = 0 if p == 0 else BS
                    low = spread[p][lo : lo + BS]
                    high = spread[p][lo + BS : lo + PAIR]
                    if p > 0:
                        tail = 2 * BS if p == 1 else 3 * BS
                        low = low + spread[p - 1][tail : tail + BS]
                    if p < HALF - 1:
                        high = high + spread[p + 1][:BS]
                    gbuf[rows(p, 0, BS)] = gbuf[rows(p, 0, BS)] + low
                    gbuf[rows(p, BS, BS)] = gbuf[rows(p, BS, BS)] + high

            def drain():
                for share in shares(layer + 2, slot):
                    sent(*share)

            if last:
                drain()
            else:
                pl.when(layer < layers - 2)(drain)
            dwst[slot] = total.astype(BF16)
            for share in shares(layer, slot):
                push(*share)

            @pl.when(layer == sec)
            def _():
                own = dwst.at[slot, pl.ds(pl.multiple_of(dom * 32, 32), 32)]
                arrived(own, dwrecv.at[giver], d_recv.at[giver])

            if not last:
                rim(slot).wait()
                gbuf[pl.ds(0, BS)] = gbuf[pl.ds(0, BS)] + grecv[slot].astype(F32)

        def backward_step(step, carry):
            backward(layers - 1 - step, False)
            return carry

        lax.fori_loop(0, layers - 1, backward_step, 0)
        backward(0, True)
        for layer in (1, 0):
            for share in shares(layer, layer % 2):
                sent(*share)

    for gift in gifts + lends + [adj] + cots:
        sent(*gift)

    total = jnp.zeros((32, dwrecv.shape[2]), F32)
    for g in range(2 * snaps):

        @pl.when(jnp.logical_not(jnp.logical_and(is_host, sec * 2 + core == g)))
        def _():
            arrived(dwrecv.at[g], dwrecv.at[g], d_recv.at[g])

        total = total + dwrecv[g].astype(F32)
    outg[dom] = total * scaling

    def gathered(k):
        return pltpu.make_async_remote_copy(
            src_ref=outg.at[dom], dst_ref=outg.at[dom],
            send_sem=o_send.at[k], recv_sem=o_recv.at[dom],
            device_id=(sec, lax.rem(dom + k + 1, 8)), device_id_type=MESH,
        )

    for k in range(7):
        gathered(k).start()
    for k in range(7):
        e = lax.rem(dom + k + 1, 8)
        arrived(outg.at[e], outg.at[e], o_recv.at[e])
    for k in range(7):
        gathered(k).wait_send()
    for e in range(8):
        out_ref[0, pl.ds(e * 32, 32)] = outg[e]


def local(features, cotangent, weights, tiles, sources, counts):
    snaps, nodes, feats = features.shape
    layers = lax.axis_size("section")
    doms = lax.axis_size("dom")
    assert (layers, doms, snaps, nodes, feats) == (16, 8, 12, 256, 256)
    scaling = 1.0 / math.sqrt(snaps * nodes * doms)
    vmem = pl.BlockSpec(memory_space=pltpu.VMEM)
    smem = pl.BlockSpec(memory_space=pltpu.SMEM)
    hbm = pl.BlockSpec(memory_space=pl.ANY)
    dma = pltpu.SemaphoreType.DMA
    return pl.pallas_call(
        functools.partial(kernel, scaling, snaps, layers),
        out_shape=jax.ShapeDtypeStruct((1, feats, feats), F32),
        in_specs=[smem, smem, vmem, vmem, hbm, hbm],
        out_specs=vmem,
        scratch_shapes=[
            pltpu.VMEM((PAIR, WIN), BF16),
            pltpu.VMEM((HALF, PAIR, WIN), BF16),
            pltpu.VMEM((HALF, WIN, PAIR), BF16),
            pltpu.VMEM((layers, feats, feats), BF16),
            pltpu.VMEM((2, ROWS + 2 * BS, feats), BF16),
            pltpu.VMEM((ROWS, feats), BF16),
            pltpu.VMEM((ROWS, feats), F32),
            pltpu.VMEM((layers, ROWS, feats), BF16),
            pltpu.VMEM((layers, ROWS, feats), F32),
            pltpu.VMEM((layers, ROWS, 128), F32),
            pltpu.VMEM((2, BS, feats), BF16),
            pltpu.VMEM((2, BS, feats), BF16),
            pltpu.VMEM((2, feats, feats), BF16),
            pltpu.VMEM((2 * snaps, 32, feats), BF16),
            pltpu.VMEM((8, 32, feats), F32),
            dma((3,)), dma((9,)), dma((3,)), dma((layers,)),
            dma, dma((HALF,)), dma((2,)), dma((8,)),
            dma((2,)), dma((2,)), dma((2,)), dma((2,)),
            dma((2, 8)), dma((2 * snaps,)), dma((7,)), dma((8,)),
        ],
        compiler_params=pltpu.CompilerParams(
            has_side_effects=True, vmem_limit_bytes=60 * 1024 * 1024
        ),
    )(sources, counts, tiles, weights, features, cotangent)


def solution(mesh):
    in_specs = (
        P(None, "dom", None),
        P(None, "dom", None),
        P("section", None, None),
        P("dom", None, None, None),
        P("dom", None),
        P("dom"),
    )
    out_specs = P("section", None, None)
    return jax.shard_map(local, mesh=mesh, in_specs=in_specs, out_specs=out_specs, check_vma=False)
```

```python
import functools
import math

import jax
import jax.numpy as jnp
from jax import lax
from jax.experimental import pallas as pl
from jax.experimental.pallas import tpu as pltpu
from jax.sharding import PartitionSpec as P

EPSILON = 1e-06
MESH = pl.DeviceIdType.MESH
F32 = jnp.float32
BF16 = jnp.bfloat16

BS = 128
PAIR = 2 * BS
WIN = 4 * BS
HALF = 4
ROWS = HALF * PAIR
AHEAD = 4


def mm(a, b):
    return jnp.dot(a, b, preferred_element_type=F32)


def mm_tn(a, b):
    return lax.dot_general(a, b, (((0,), (0,)), ((), ())), preferred_element_type=F32)


def mm_nt(a, b):
    return lax.dot_general(a, b, (((1,), (1,)), ((), ())), preferred_element_type=F32)


def rows(p, offset=0, size=PAIR):
    return pl.ds(p * PAIR + offset, size)


def kernel(
    scaling, snaps, layers,
    src_ref, cnt_ref, tiles_ref, w_ref, feat_ref, cot_ref, out_ref,
    asend, abuf, atbuf, wbuf, hbuf, cotb, gbuf, nrmb, dsb, scb,
    gsend, grecv, keep, lent, fetched, dwst, dwrecv, outg,
    f_send, f_recv, w_send, w_recv, a_send, a_recv, c_send, c_recv,
    v_send, v_recv, h_send, h_recv, g_send, g_recv, p_send, p_recv,
    d_send, d_recv, o_send, o_recv,
):
    sec = lax.axis_index("section")
    dom = lax.axis_index("dom")
    x, core = dom // 2, dom % 2
    active = sec < snaps
    host_x = lax.rem(sec // 4 + lax.rem(sec, 4), 4)
    is_host = jnp.logical_and(active, x == host_x)
    half = dom // 4
    mirrored = half == 0
    place = jnp.where(mirrored, 3 - dom, dom - 4)
    target = host_x * 2 + half
    other = host_x * 2 + 1 - half
    partner = x * 2 + 1 - core
    slots = [jnp.where(mirrored, 1 - j, j) for j in range(2)]

    barrier = pltpu.get_barrier_semaphore()
    for k in range(1, 8):
        pl.semaphore_signal(
            barrier, inc=1, device_id=(sec, lax.rem(dom + k, 8)), device_id_type=MESH
        )

    @pl.when(is_host)
    def _():
        for k in range(1, 16):
            pl.semaphore_signal(
                barrier, inc=1, device_id=(lax.rem(sec + k, 16), dom), device_id_type=MESH
            )

    def push(src, dst, send, recv, to_sec, to_dom, guard):
        here = jnp.logical_and(to_sec == sec, to_dom == dom)

        @pl.when(jnp.logical_and(guard, here))
        def _():
            pltpu.make_async_copy(src, dst, recv).start()

        @pl.when(jnp.logical_and(guard, jnp.logical_not(here)))
        def _():
            pltpu.make_async_remote_copy(
                src_ref=src, dst_ref=dst, send_sem=send, recv_sem=recv,
                device_id=(to_sec, to_dom), device_id_type=MESH,
            ).start()

    def sent(src, dst, send, recv, to_sec, to_dom, guard):
        here = jnp.logical_and(to_sec == sec, to_dom == dom)

        @pl.when(jnp.logical_and(guard, jnp.logical_not(here)))
        def _():
            pltpu.make_async_remote_copy(
                src_ref=src, dst_ref=dst, send_sem=send, recv_sem=recv,
                device_id=(to_sec, to_dom), device_id_type=MESH,
            ).wait_send()

    def arrived(src, dst, recv):
        pltpu.make_async_copy(src, dst, recv).wait()

    def block(q):
        return pl.ds(pl.multiple_of(q * BS, BS), BS)

    @pl.when(active)
    def _():
        first = 2 * dom - 1
        for b in range(2):
            want = []
            for k in range(6):
                loc = src_ref[b, k] - first
                loc = jnp.where(mirrored, 3 - loc, loc)
                want.append(jnp.where(k < cnt_ref[b], loc, -1))
            parts = []
            for c in range(4):
                total = jnp.zeros((BS, BS), F32)
                for k in range(6):
                    keep = jnp.where(want[k] == c, 1.0, 0.0).astype(F32)
                    total = total + tiles_ref[b, k].astype(F32) * keep
                parts.append(total)
            degree = jnp.sum(parts[0] + parts[1] + parts[2] + parts[3], axis=-1, keepdims=True)
            scale = 1.0 / degree
            for c in range(4):
                asend[block(slots[b]), pl.ds(c * BS, BS)] = (parts[c] * scale).astype(BF16)

    pl.semaphore_wait(barrier, jnp.where(is_host, 9, 10))

    gifts = []
    for j in range(2):
        q = 2 * place + slots[j]
        gifts.append((
            feat_ref.at[jnp.minimum(sec, snaps - 1), pl.ds(j * BS, BS)], hbuf.at[0, block(q + 1)],
            f_send.at[j], f_recv.at[q], sec, target, active,
        ))
    edge = jnp.where(mirrored, 1, 0)
    gifts.append((
        feat_ref.at[jnp.minimum(sec, snaps - 1), block(edge)], hbuf.at[0, pl.ds(0, BS)],
        f_send.at[2], f_recv.at[8], sec, other,
        jnp.logical_and(active, jnp.logical_or(dom == 3, dom == 4)),
    ))
    for gift in gifts:
        push(*gift)
    adj = (asend, abuf.at[place], a_send, a_recv.at[place], sec, target, active)
    push(*adj)
    cots = []
    for j in range(2):
        q = 2 * place + slots[j]
        cots.append((
            cot_ref.at[jnp.minimum(sec, snaps - 1), pl.ds(j * BS, BS)], cotb.at[block(q)],
            c_send.at[j], c_recv.at[q], sec, target, active,
        ))

    mine = block(core)
    lends = []
    for j in range(3):
        to_sec = 4 * j + lax.rem(x - j + 4, 4)
        lends.append((
            w_ref.at[0, mine], wbuf.at[sec, mine], w_send.at[j], w_recv.at[sec], to_sec, dom, True,
        ))
    for lend in lends:
        push(*lend)
    for cot in cots:
        push(*cot)

    @pl.when(is_host)
    def _():
        for s in range(2):
            hbuf[s, pl.ds(ROWS + BS, BS)] = jnp.zeros((BS, hbuf.shape[2]), BF16)
        def swap(layer):
            return pltpu.make_async_remote_copy(
                src_ref=wbuf.at[layer, mine], dst_ref=wbuf.at[layer, mine],
                send_sem=v_send.at[layer], recv_sem=v_recv.at[layer],
                device_id=(sec, partner), device_id_type=MESH,
            )

        def relay(layer):
            arrived(wbuf.at[layer, mine], wbuf.at[layer, mine], w_recv.at[layer])
            swap(layer).start()

        for layer in range(AHEAD):
            relay(layer)
        for q in range(9):
            dst = hbuf.at[0, pl.ds((q + 1) % 9 * BS, BS)]
            arrived(dst, dst, f_recv.at[q])
        for p in range(HALF):
            arrived(abuf.at[p], abuf.at[p], a_recv.at[p])

        def halo(slot):
            return pltpu.make_async_remote_copy(
                src_ref=hbuf.at[slot, pl.ds(BS, BS)], dst_ref=hbuf.at[slot, pl.ds(0, BS)],
                send_sem=h_send.at[slot], recv_sem=h_recv.at[slot],
                device_id=(sec, partner), device_id_type=MESH,
            )

        def forward(layer, last):
            now = lax.rem(layer, 2)
            later = 1 - now
            if not last:

                @pl.when(layer < layers - AHEAD)
                def _():
                    relay(layer + AHEAD)

            theirs = block(1 - core)
            arrived(wbuf.at[layer, theirs], wbuf.at[layer, theirs], v_recv.at[layer])
            if last:
                halo(now).wait_recv()
            else:

                @pl.when(layer > 0)
                def _():
                    halo(now).wait_recv()

            for p in range(HALF):
                agg = mm(abuf[p], hbuf[now, pl.ds(p * PAIR, WIN)])
                scale = lax.rsqrt(jnp.mean(agg * agg, axis=-1, keepdims=True) + EPSILON)
                nrm = (agg * scale).astype(BF16)
                nrmb[layer, rows(p)] = nrm
                scb[layer, rows(p)] = jnp.broadcast_to(scale, (PAIR, 128))
                hz = 0.5 * mm(nrm, wbuf[layer])
                t = jnp.tanh(hz)
                u = 1.0 + t
                dsb[layer, rows(p)] = (0.5 * u) * (1.0 + hz * (1.0 - t))
                if not last:
                    old = hbuf[now, rows(p, BS)].astype(F32)
                    hbuf[later, rows(p, BS)] = (old + hz * u).astype(BF16)
                    if p == 0:
                        halo(later).start()
            if not last:
                halo(later).wait_send()

        def forward_step(layer, carry):
            forward(layer, False)
            return carry

        lax.fori_loop(0, layers - 1, forward_step, 0)
        forward(layers - 1, True)

        for p in range(HALF):
            atbuf[p] = abuf[p].T
        for q in range(8):
            arrived(cotb.at[pl.ds(q * BS, BS)], cotb.at[pl.ds(q * BS, BS)], c_recv.at[q])
        gbuf[...] = cotb[...].astype(F32)

        def rim(slot):
            return pltpu.make_async_remote_copy(
                src_ref=gsend.at[slot], dst_ref=grecv.at[slot],
                send_sem=g_send.at[slot], recv_sem=g_recv.at[slot],
                device_id=(sec, partner), device_id_type=MESH,
            )

        def joint(layer):
            return pltpu.make_async_remote_copy(
                src_ref=lent.at[layer], dst_ref=fetched.at[layer],
                send_sem=p_send.at[layer], recv_sem=p_recv.at[layer],
                device_id=(sec, partner), device_id_type=MESH,
            )

        def shares(layer):
            return [
                (
                    dwst.at[layer, pl.ds(e * 32, 32)], dwrecv.at[sec],
                    d_send.at[layer, e], d_recv.at[sec], layer, core * 4 + e, True,
                )
                for e in range(4)
            ]

        def deliver(layer):
            joint(layer).wait_recv()
            both = keep[lax.rem(layer, 2)] + fetched[layer].astype(F32)
            dwst[layer] = both.astype(BF16)
            for share in shares(layer):
                push(*share)

        def backward(layer, last):
            slot = lax.rem(layer, 2)
            total = None
            daggs = []
            for p in range(HALF):
                dz = (gbuf[rows(p)] * dsb[layer, rows(p)]).astype(BF16)
                nrm = nrmb[layer, rows(p)]
                if not last:
                    dnrm = mm_nt(dz, wbuf[layer])
                    wide = nrm.astype(F32)
                    mean = jnp.mean(dnrm * wide, axis=-1, keepdims=True)
                    scale = scb[layer, rows(p)][:, :1]
                    dagg = (scale * (dnrm - wide * mean)).astype(BF16)
                    daggs.append(dagg)
                    if p == 0:
                        gsend[slot] = mm(atbuf[0, pl.ds(0, BS)], dagg).astype(BF16)
                        rim(slot).start()
                term = mm_tn(nrm, dz)
                total = term if total is None else total + term
            if not last:
                spread = [mm(atbuf[0, pl.ds(BS, WIN - BS)], daggs[0])]
                spread += [mm(atbuf[p], daggs[p]) for p in range(1, HALF)]
                for p in range(HALF):
                    lo = 0 if p == 0 else BS
                    low = spread[p][lo : lo + BS]
                    high = spread[p][lo + BS : lo + PAIR]
                    if p > 0:
                        tail = 2 * BS if p == 1 else 3 * BS
                        low = low + spread[p - 1][tail : tail + BS]
                    if p < HALF - 1:
                        high = high + spread[p + 1][:BS]
                    gbuf[rows(p, 0, BS)] = gbuf[rows(p, 0, BS)] + low
                    gbuf[rows(p, BS, BS)] = gbuf[rows(p, BS, BS)] + high

            total = jnp.where(core == 0, total, jnp.concatenate([total[BS:], total[:BS]], axis=0))
            keep[slot] = total[:BS]
            lent[layer] = total[BS:].astype(BF16)
            joint(layer).start()
            if last:
                deliver(1)
                deliver(0)
            else:

                @pl.when(layer < layers - 1)
                def _():
                    deliver(layer + 1)

            if not last:
                rim(slot).wait()
                gbuf[pl.ds(0, BS)] = gbuf[pl.ds(0, BS)] + grecv[slot].astype(F32)

        def backward_step(step, carry):
            backward(layers - 1 - step, False)
            return carry

        lax.fori_loop(0, layers - 1, backward_step, 0)
        backward(0, True)

        def settle(layer, carry):
            swap(layer).wait_send()
            joint(layer).wait_send()
            for share in shares(layer):
                sent(*share)
            return carry

        lax.fori_loop(0, layers, settle, 0)

    for gift in gifts + lends + [adj] + cots:
        sent(*gift)

    total = jnp.zeros((32, dwrecv.shape[2]), F32)
    for g in range(snaps):
        arrived(dwrecv.at[g], dwrecv.at[g], d_recv.at[g])
        total = total + dwrecv[g].astype(F32)
    outg[dom] = (total * scaling).astype(BF16)

    def gathered(k):
        return pltpu.make_async_remote_copy(
            src_ref=outg.at[dom], dst_ref=outg.at[dom],
            send_sem=o_send.at[k], recv_sem=o_recv.at[dom],
            device_id=(sec, lax.rem(dom + k + 1, 8)), device_id_type=MESH,
        )

    for k in range(7):
        gathered(k).start()
    for k in range(7):
        e = lax.rem(dom + k + 1, 8)
        arrived(outg.at[e], outg.at[e], o_recv.at[e])
    for k in range(7):
        gathered(k).wait_send()
    for e in range(8):
        out_ref[0, pl.ds(e * 32, 32)] = outg[e].astype(F32)


def local(features, cotangent, weights, tiles, sources, counts):
    snaps, nodes, feats = features.shape
    layers = lax.axis_size("section")
    doms = lax.axis_size("dom")
    assert (layers, doms, snaps, nodes, feats) == (16, 8, 12, 256, 256)
    scaling = 1.0 / math.sqrt(snaps * nodes * doms)
    vmem = pl.BlockSpec(memory_space=pltpu.VMEM)
    smem = pl.BlockSpec(memory_space=pltpu.SMEM)
    hbm = pl.BlockSpec(memory_space=pl.ANY)
    dma = pltpu.SemaphoreType.DMA
    return pl.pallas_call(
        functools.partial(kernel, scaling, snaps, layers),
        out_shape=jax.ShapeDtypeStruct((1, feats, feats), F32),
        in_specs=[smem, smem, vmem, vmem, hbm, hbm],
        out_specs=vmem,
        scratch_shapes=[
            pltpu.VMEM((PAIR, WIN), BF16),
            pltpu.VMEM((HALF, PAIR, WIN), BF16),
            pltpu.VMEM((HALF, WIN, PAIR), BF16),
            pltpu.VMEM((layers, feats, feats), BF16),
            pltpu.VMEM((2, ROWS + 2 * BS, feats), BF16),
            pltpu.VMEM((ROWS, feats), BF16),
            pltpu.VMEM((ROWS, feats), F32),
            pltpu.VMEM((layers, ROWS, feats), BF16),
            pltpu.VMEM((layers, ROWS, feats), F32),
            pltpu.VMEM((layers, ROWS, 128), F32),
            pltpu.VMEM((2, BS, feats), BF16),
            pltpu.VMEM((2, BS, feats), BF16),
            pltpu.VMEM((2, BS, feats), F32),
            pltpu.VMEM((layers, BS, feats), BF16),
            pltpu.VMEM((layers, BS, feats), BF16),
            pltpu.VMEM((layers, BS, feats), BF16),
            pltpu.VMEM((snaps, 32, feats), BF16),
            pltpu.VMEM((8, 32, feats), BF16),
            dma((3,)), dma((9,)), dma((3,)), dma((layers,)),
            dma, dma((HALF,)), dma((2,)), dma((8,)),
            dma((layers,)), dma((layers,)),
            dma((2,)), dma((2,)), dma((2,)), dma((2,)), dma((layers,)), dma((layers,)),
            dma((layers, 4)), dma((snaps,)), dma((7,)), dma((8,)),
        ],
        compiler_params=pltpu.CompilerParams(
            collective_id=0, has_side_effects=True, vmem_limit_bytes=60 * 1024 * 1024
        ),
    )(sources, counts, tiles, weights, features, cotangent)


def solution(mesh):
    in_specs = (
        P(None, "dom", None),
        P(None, "dom", None),
        P("section", None, None),
        P("dom", None, None, None),
        P("dom", None),
        P("dom"),
    )
    out_specs = P("section", None, None)
    return jax.shard_map(local, mesh=mesh, in_specs=in_specs, out_specs=out_specs, check_vma=False)
```
